256 devices in a mesh: types: 128 (over x, z, y), tm: 2 (over core).
Axes of the slice: x: 4, y: 4, z: 8, core: 2. Of those that a mesh axis runs over, the one named last changes fastest.
Arguments:
- brackets: int32 [768, 8, 7, 512], P('types', 'tm'), may hold values from 0 to 510, as said below
- active_blocks: int32 [768], P('types'), may hold values from 1 to 4, as said below
- initial_mass: float32 [768, 7, 512], P('types'), may hold values from 0 to 0.00055803574
- patience: float32 [768], P('types'), may hold values from 0.9 to 0.985
- productivity: float32 [768], P('types'), may hold values from 0.5 to 2
- income_levels: float32 [7], replicated, may hold values from 0.3 to 3
- income_transition: float32 [7, 7], replicated, may hold values from 0 to 1, as said below
- wage_path: float32 [8], replicated, may hold values from 0.8 to 1.2
- bond_supply: float32 [8], replicated, may hold values from 0.5 to 2
- price_guess: float32 [8], replicated, may hold values from -3 to 3
- jac_inverse: float32 [8, 8], replicated, may hold values from -2 to 2
- assignment: int32 [768], replicated, may hold values from 0 to 767, each once
Outputs:
- price_path: float32 [8], replicated
- market_gap: float32 [8], replicated
- type_paths: float32 [768, 2, 8], P('types')
The draws below stay inside these ranges and needn't reach their ends.
Inputs may be any that keep to these rules, and one draw needn't show every extreme that they name: `brackets`: the bracket of asset point i lies between max(i - 9, 0) and max(i - 1, 0). `active_blocks`: counts of 128-point blocks from the bottom of the grid. `income_transition`: rows of positive entries summing to one. `assignment`: each type appears once.
All inputs are finite; a program needn't handle non-finite values.
Results may differ from the reference program's by a relative error of at most 0.0003.
Values sent between devices are 32-bit elements; how exact they have to be, the bound alone decides.
No kernel may reach another device: no remote copies, remote signals or barrier semaphores. Data moves between devices by JAX's collectives and lax.ppermute only.
A program may use at most 64 MiB of HBM per device.

```python
import math
import jax
import jax.numpy as jnp
from jax import lax

ASSETS = 512
INCOME = 7
BLOCK = 128
REACH = 8
NEWTON = 2
TYPES_DEV = 6
TYPES = 768
PERIODS = 8


def draw_brackets(key, part):
    points = jnp.arange(ASSETS, dtype=jnp.int32)
    drop_sizes = jax.random.randint(key, (TYPES, PERIODS, INCOME, ASSETS), 0, REACH + 1)
    return jnp.maximum(points - 1 - drop_sizes, 0).astype(jnp.int32)


def draw_active_blocks(key, part):
    largest = ASSETS // BLOCK
    groups = TYPES // TYPES_DEV
    heavy_key = jax.random.fold_in(key, 11)
    pick_key = jax.random.fold_in(key, 12)
    jitter_key = jax.random.fold_in(key, 13)
    full_key = jax.random.fold_in(key, 14)
    heavy_group = jax.random.randint(heavy_key, (groups,), 0, 4) == 0
    heavy_group = heavy_group.at[jax.random.randint(pick_key, (), 0, groups)].set(True)
    heavy_rows = jnp.repeat(heavy_group, TYPES_DEV)
    jitter = jax.random.randint(jitter_key, (TYPES,), 0, 2)
    counts = jnp.where(heavy_rows, largest - 1 + jitter, 1 + jitter)
    counts = counts.at[jax.random.randint(full_key, (), 0, TYPES)].set(largest)
    return counts.astype(jnp.int32)


def draw_income_transition(key, part):
    raw_values = jax.random.uniform(key, (INCOME, INCOME), jnp.float32, 0.2, 1.0) + 2.0 * jnp.eye(INCOME, dtype=jnp.float32)
    return raw_values / jnp.sum(raw_values, axis=1, keepdims=True)


def level_of(key, shape, split, smallest, top_value):
    level = 1.0
    for axis_at, blocks in split:
        heights = jax.random.uniform(jax.random.fold_in(jax.random.fold_in(key, 6), axis_at), (blocks,), jnp.float32, smallest / len(split), top_value / len(split))
        level = level * jnp.repeat(jnp.exp(heights), shape[axis_at] // blocks).reshape((-1,) + (1,) * (len(shape) - 1 - axis_at))
    return level


def centred(own_key, dims, scale, bound, kind=jnp.bfloat16):
    entries = scale * jax.random.normal(own_key, dims, jnp.float32)
    return jnp.clip(entries, min=-bound, max=bound).astype(kind)


def setup_inputs(seed: int = 0) -> dict:
    keys = jax.random.split(jax.random.key(seed), 13)
    return {
        "brackets": draw_brackets(jax.random.fold_in(keys[12], 71), 0),
        "active_blocks": draw_active_blocks(jax.random.fold_in(keys[12], 71), 0),
        "initial_mass": jnp.clip(0.00055803574 * jax.random.uniform(keys[2], (TYPES, INCOME, ASSETS), jnp.float32) ** level_of(keys[2], (TYPES, INCOME, ASSETS), ((0, 128),), -0.2, 0.2), 0.0, 0.00055803574),
        "patience": jnp.clip(0.9 + 0.08500004 * jax.random.uniform(keys[3], (TYPES,), jnp.float32) ** level_of(keys[3], (TYPES,), ((0, 128),), -0.2, 0.2), 0.9, 0.985),
        "productivity": jnp.clip(jnp.exp(math.log(2.0) - 1.3862944 * jax.random.uniform(keys[4], (TYPES,), jnp.float32) ** level_of(keys[4], (TYPES,), ((0, 128),), -0.2, 0.2)), 0.5, 2.0),
        "income_levels": jnp.clip(jnp.exp(jax.random.uniform(keys[5], (INCOME,), jnp.float32, math.log(0.3), math.log(3.0))), 0.3, 3.0),
        "income_transition": draw_income_transition(jax.random.fold_in(keys[12], 71), 0),
        "wage_path": jnp.clip(jax.random.uniform(keys[7], (PERIODS,), jnp.float32, 0.8, 1.2), 0.8, 1.2),
        "bond_supply": jnp.clip(jax.random.uniform(keys[8], (PERIODS,), jnp.float32, 0.5, 2.0), 0.5, 2.0),
        "price_guess": centred(keys[9], (PERIODS,), 1.0, 3.0, jnp.float32),
        "jac_inverse": centred(keys[10], (PERIODS, PERIODS), PERIODS ** -0.5, 2.0, jnp.float32),
        "assignment": jax.random.permutation(keys[11], TYPES).astype(jnp.int32),
    }


grid_top = 40.0
rate_floor = 0.005
rate_span = 0.03
highest = lax.Precision.HIGHEST


def asset_grid(points):
    return grid_top * (points / (ASSETS - 1)) ** 2


def interest(price_path):
    return rate_floor + rate_span * jax.nn.sigmoid(price_path)


def policy(lower_edge, upper_edge, bracket_now, rate_now, income_now, grid_rows):
    grid_low = asset_grid(bracket_now.astype(jnp.float32))
    grid_high = asset_grid((bracket_now + 1).astype(jnp.float32))
    spacing = jnp.maximum(upper_edge - lower_edge, (grid_high - grid_low) / (1.0 + rate_now))
    weight_up = jnp.clip((grid_rows[None, :] - lower_edge) / spacing, 0.0, 1.0)
    savings = grid_low + weight_up * (grid_high - grid_low)
    spending = (1.0 + rate_now) * grid_rows[None, :] + income_now[:, None] - savings
    return weight_up, savings, spending


def solve_type(bracket, mass_start, blocks, patience, productivity, interest_path, wage_path, income_levels, transition):
    grid_values = asset_grid(jnp.arange(ASSETS, dtype=jnp.float32))
    incomes = wage_path[:, None] * productivity * income_levels[None, :]
    last_rate = interest_path[-1]
    values_end = (1.0 + last_rate) / (last_rate * grid_values[None, :] + incomes[-1][:, None])

    def backward(values, inputs):
        bracket_now, rate_now, income_now = inputs
        expected = patience * jnp.dot(transition, values, precision=highest)
        endogenous = (1.0 / expected + grid_values[None, :] - income_now[:, None]) / (1.0 + rate_now)
        lower_edge = jnp.take_along_axis(endogenous, bracket_now, axis=1)
        upper_edge = jnp.take_along_axis(endogenous, bracket_now + 1, axis=1)
        weight_up, savings, spending = policy(lower_edge, upper_edge, bracket_now, rate_now, income_now, grid_values)
        return (1.0 + rate_now) / spending, (weight_up, savings, spending)

    values_start, policies = lax.scan(backward, values_end, (bracket, interest_path, incomes), reverse=True)
    live_rows = (jnp.arange(ASSETS, dtype=jnp.int32) < blocks * BLOCK).astype(jnp.float32)
    masses = mass_start * live_rows[None, :]

    def spread(target_row, staying, rising):
        empty = jnp.zeros((ASSETS,), jnp.float32)
        return empty.at[target_row].add(staying).at[target_row + 1].add(rising)

    def forward(masses, inputs):
        bracket_now, weight_up, savings, spending = inputs
        totals = jnp.stack([jnp.sum(masses * savings), jnp.sum(masses * spending)])
        arrived = jax.vmap(spread)(bracket_now, (1.0 - weight_up) * masses, weight_up * masses)
        return jnp.dot(transition.T, arrived, precision=highest), totals

    masses_end, type_series = lax.scan(forward, masses, (bracket, policies[0], policies[1], policies[2]))
    return type_series.T


def reference(brackets, active_blocks, initial_mass, patience, productivity, income_levels, income_transition, wage_path, bond_supply, price_guess, jac_inverse, assignment):
    price_path = price_guess
    market_gap = jnp.zeros_like(price_guess)
    type_series = jnp.zeros((TYPES, 2, PERIODS), jnp.float32)
    for newton_round in range(NEWTON):
        interest_path = interest(price_path)

        def solve_member(members):
            return solve_type(members[0], members[1], members[2], members[3], members[4], interest_path, wage_path, income_levels, income_transition)

        type_series = lax.map(solve_member, (brackets, initial_mass, active_blocks, patience, productivity))
        totals = jnp.sum(type_series[:, 0, :], axis=0)
        market_gap = totals / TYPES - bond_supply
        price_path = price_path - jnp.dot(jac_inverse, market_gap, precision=highest)
    type_paths = type_series[assignment]
    return price_path, market_gap, type_paths
```

```python
import functools

import jax
import jax.numpy as jnp
from jax import lax
from jax.experimental import pallas as pl
from jax.experimental.pallas import tpu as pltpu
from jax.sharding import Mesh
from jax.sharding import PartitionSpec as P

ASSETS = 512
INCOME = 7
BLOCK = 128
REACH = 8
PERIODS = 8
HALF = PERIODS // 2
BLOCKS = ASSETS // BLOCK
ROWS = 16
TYPES = ("types_0", "types_1", "types_2")
EVERY = ("types_0", "types_1", "types_2", "tm")

grid_top = 40.0
grid_scale = grid_top / (ASSETS - 1) ** 2
rate_floor = 0.005
rate_span = 0.03

VMEM = pl.BlockSpec(memory_space=pltpu.VMEM)
SMEM = pl.BlockSpec(memory_space=pltpu.SMEM)


def iota(dim, shape=(ROWS, BLOCK)):
    return lax.broadcasted_iota(jnp.int32, shape, dim)


def by_type(scalars):
    kind = iota(0) // BLOCKS
    value = jnp.full((ROWS, BLOCK), scalars[-1], jnp.float32)
    for k in range(len(scalars) - 2, -1, -1):
        value = jnp.where(kind == k, scalars[k], value)
    return value


def diagonal():
    return iota(0, (PERIODS, PERIODS)) == iota(1, (PERIODS, PERIODS))


def gap_row(totals_row, supply_row, all_types):
    return totals_row * (1.0 / all_types) - supply_row


def price_column(price_row, jac, gaps):
    wide = jnp.where(diagonal(), jnp.broadcast_to(price_row, (PERIODS, PERIODS)), 0.0)
    for gap in gaps:
        wide = wide - jac * gap
    return jnp.sum(wide, axis=1, keepdims=True)


def set_rates(price, rates):
    rate = rate_floor + rate_span / (1.0 + jnp.exp(-price))
    rate = jnp.broadcast_to(rate, (PERIODS, BLOCK))
    rates[0] = rate
    rates[1] = 1.0 / (1.0 + rate)


def solve(core, half_types, patience, productivity, levels, transition, wage, brackets, start, rates, weights, savings, series, full):
    lane, row = iota(1), iota(0)
    point = (row % BLOCKS) * BLOCK + lane
    first = (row % BLOCKS) * BLOCK
    grid = point.astype(jnp.float32)
    grid = grid_scale * grid * grid
    types = [core * half_types + k for k in range(half_types)]
    beta = by_type([patience[k] for k in types])
    skill = by_type([productivity[k] for k in types])
    mixing = [[transition[e, f] for f in range(INCOME)] for e in range(INCOME)]
    pay = [levels[e] for e in range(INCOME)]

    def rate_at(t):
        rate = jnp.broadcast_to(rates[0, pl.ds(t, 1), :], (ROWS, BLOCK))
        inverse = jnp.broadcast_to(rates[1, pl.ds(t, 1), :], (ROWS, BLOCK))
        return rate, inverse

    last, _ = rate_at(PERIODS - 1)
    values = tuple((1.0 + last) / (last * grid + (wage[PERIODS - 1] * pay[e]) * skill) for e in range(INCOME))

    def backward(step, values):
        t = PERIODS - 1 - step
        rate, inverse = rate_at(t)
        budget = (1.0 + rate) * grid
        fresh = []
        for e in range(INCOME):
            mixed = mixing[e][0] * values[0]
            for f in range(1, INCOME):
                mixed = mixed + mixing[e][f] * values[f]
            income = (wage[t] * pay[e]) * skill
            edge = (1.0 / (beta * mixed) + grid - income) * inverse
            above = pltpu.roll(edge, 1, 0)
            bracket = brackets[t, e]
            spot, after = bracket & (BLOCK - 1), (bracket + 1) & (BLOCK - 1)
            lower = jnp.where(
                bracket >= first,
                jnp.take_along_axis(edge, spot, axis=1),
                jnp.take_along_axis(above, spot, axis=1),
            )
            upper = jnp.where(
                bracket + 1 >= first,
                jnp.take_along_axis(edge, after, axis=1),
                jnp.take_along_axis(above, after, axis=1),
            )
            place = bracket.astype(jnp.float32)
            low = grid_scale * place * place
            width = grid_scale * (2.0 * place + 1.0)
            spacing = jnp.maximum(upper - lower, width * inverse)
            weight = jnp.clip((grid - lower) / spacing, 0.0, 1.0)
            saved = low + weight * width
            weights[t, e] = weight
            savings[t, e] = saved
            fresh.append((1.0 + rate) / (budget + income - saved))
        return tuple(fresh)

    lax.fori_loop(0, PERIODS, backward, values)

    def sums(t, masses):
        rate, _ = rate_at(t)
        budget = (1.0 + rate) * grid
        assets = jnp.zeros((ROWS, BLOCK), jnp.float32)
        spent = jnp.zeros((ROWS, BLOCK), jnp.float32)
        for e in range(INCOME):
            saved = savings[t, e]
            assets = assets + masses[e] * saved
            if full:
                spent = spent + masses[e] * (budget + (wage[t] * pay[e]) * skill - saved)
        series[0, t] = assets
        if full:
            series[1, t] = spent

    def forward(t, masses):
        sums(t, masses)
        arrived = []
        for e in range(INCOME):
            weight = weights[t, e]
            rising = weight * masses[e]
            staying = (1.0 - weight) * masses[e]
            drop = point - brackets[t, e]
            hit = [drop == s for s in range(REACH + 2)]
            here = jnp.where(hit[0], staying, jnp.where(hit[1], rising, 0.0))
            here = here + pltpu.roll(jnp.where(hit[0], rising, 0.0), 1, 1)
            crossed = jnp.zeros((ROWS, BLOCK), jnp.float32)
            for s in range(1, REACH + 2):
                moved = jnp.where(hit[s], staying, jnp.where(hit[s + 1], rising, 0.0) if s <= REACH else 0.0)
                moved = pltpu.roll(moved, BLOCK - s, 1)
                inside = lane < BLOCK - s
                here = here + jnp.where(inside, moved, 0.0)
                crossed = crossed + jnp.where(inside, 0.0, moved)
            arrived.append(here + pltpu.roll(crossed, ROWS - 1, 0))
        fresh = []
        for f in range(INCOME):
            mixed = mixing[0][f] * arrived[0]
            for e in range(1, INCOME):
                mixed = mixed + mixing[e][f] * arrived[e]
            fresh.append(mixed)
        return tuple(fresh)

    masses = tuple(start[e] for e in range(INCOME))
    masses = lax.fori_loop(0, PERIODS - 1, forward, masses)
    sums(PERIODS - 1, masses)


def lane_sums(arrays):
    lane = iota(1)
    held = jnp.zeros((ROWS, BLOCK), jnp.float32)
    for q, array in enumerate(arrays):
        held = jnp.where(lane == q, jnp.sum(array, axis=1, keepdims=True), held)
    return held


def first_kernel(
    blocks, patience, productivity, levels, transition, wage, split, mass, price,
    out, brackets, start, rates, weights, savings, series,
):
    half_types = split.shape[1]
    core = lax.axis_index("tm")
    for k in range(half_types):
        alive = blocks[core * half_types + k]
        for e in range(INCOME):
            for b in range(BLOCKS):
                line = pl.ds(k * BLOCKS + b, 1)
                part = pl.ds(b * BLOCK, BLOCK)
                live = (b < alive).astype(jnp.float32)
                start[e, line, :] = mass[core * half_types + k, pl.ds(e, 1), part] * live
                for t in range(PERIODS):
                    brackets[t, e, line, :] = split[t // HALF, k, e, pl.ds(t % HALF, 1), part]
    spare = ROWS - half_types * BLOCKS
    for e in range(INCOME):
        start[e, ROWS - spare :, :] = jnp.zeros((spare, BLOCK), jnp.float32)
        for t in range(PERIODS):
            brackets[t, e, ROWS - spare :, :] = brackets[t, e, ROWS - 2 * spare : ROWS - spare, :]
    set_rates(price_column(price[...], None, ()), rates)
    solve(core, half_types, patience, productivity, levels, transition, wage, brackets, start, rates, weights, savings, series, False)
    held = lane_sums([series[0, t] for t in range(PERIODS)])
    total = jnp.sum(held, axis=0, keepdims=True)[:, :PERIODS]
    out[...] = jnp.broadcast_to(total, out.shape)


def second_kernel(
    patience, productivity, levels, transition, wage, brackets, start, price, jac, supply, totals,
    out, gap_out, rates, weights, savings, series,
    *, half_types, all_types,
):
    core = lax.axis_index("tm")
    total = jnp.sum(totals[...], axis=0, keepdims=True)
    gap = gap_row(total, supply[...], all_types)
    gap_out[...] = gap
    set_rates(price_column(price[...], jac[...], (gap,)), rates)
    solve(core, half_types, patience, productivity, levels, transition, wage, brackets, start, rates, weights, savings, series, True)
    held = lane_sums([series[c, t] for c in range(2) for t in range(PERIODS)])
    for k in range(half_types):
        line = jnp.sum(held[k * BLOCKS : (k + 1) * BLOCKS], axis=0, keepdims=True)
        width = 2 * PERIODS
        out[:, k * width : (k + 1) * width] = jnp.broadcast_to(line[:, :width], (out.shape[0], width))


def last_kernel(assignment, price, jac, supply, first_gap, everything, price_out, gap_out, paths_out, *, half_types, all_types):
    here = lax.axis_index(TYPES)
    width = 2 * PERIODS
    total = jnp.sum(everything[...], axis=0, keepdims=True)
    assets = total[:, :PERIODS]
    for k in range(1, half_types):
        assets = assets + total[:, k * width : k * width + PERIODS]
    gap = gap_row(assets, supply[...], all_types)
    gap_out[...] = gap
    column = price_column(price[...], jac[...], (first_gap[...], gap))
    price_out[...] = jnp.sum(jnp.where(diagonal(), column, 0.0), axis=0, keepdims=True)
    slots = paths_out.shape[0]
    for s in range(slots):
        wanted = assignment[here * slots + s]
        line = everything[pl.ds(wanted // half_types, 1), :]
        kind = wanted % half_types
        found = line[:, :width]
        for k in range(1, half_types):
            found = jnp.where(kind == k, line[:, k * width : (k + 1) * width], found)
        for c in range(2):
            paths_out[s, pl.ds(c, 1), :] = found[:, c * PERIODS : (c + 1) * PERIODS]


def body(
    brackets,
    active_blocks,
    initial_mass,
    patience,
    productivity,
    income_levels,
    income_transition,
    wage_path,
    bond_supply,
    price_guess,
    jac_inverse,
    assignment,
):
    local_types = patience.shape[0]
    all_types = local_types * lax.axis_size(TYPES)
    cores = lax.axis_size("tm")
    devices = lax.axis_size(EVERY)
    half_types = local_types // cores
    f32, i32 = jnp.float32, jnp.int32
    shape = jax.ShapeDtypeStruct
    by_income = jnp.transpose(brackets, (0, 2, 1, 3)).reshape(cores, half_types, INCOME, HALF, ASSETS)
    split = lax.all_to_all(by_income, "tm", split_axis=0, concat_axis=0, tiled=True)
    price_row = price_guess.reshape(1, PERIODS)
    supply_row = bond_supply.reshape(1, PERIODS)
    work = [
        pltpu.VMEM((2, PERIODS, BLOCK), f32),
        pltpu.VMEM((PERIODS, INCOME, ROWS, BLOCK), f32),
        pltpu.VMEM((PERIODS, INCOME, ROWS, BLOCK), f32),
        pltpu.VMEM((2, PERIODS, ROWS, BLOCK), f32),
    ]
    sent, by_row, start = pl.pallas_call(
        first_kernel,
        name="first_round",
        out_shape=(
            shape((devices, PERIODS), f32),
            shape((PERIODS, INCOME, ROWS, BLOCK), i32),
            shape((INCOME, ROWS, BLOCK), f32),
        ),
        in_specs=[SMEM] * 6 + [VMEM] * 3,
        out_specs=(VMEM,) * 3,
        scratch_shapes=work,
    )(active_blocks, patience, productivity, income_levels, income_transition, wage_path, split, initial_mass, price_row)
    totals = lax.all_to_all(sent, EVERY, split_axis=0, concat_axis=0, tiled=True)
    sent, first_gap = pl.pallas_call(
        functools.partial(second_kernel, half_types=half_types, all_types=all_types),
        name="second_round",
        out_shape=(shape((devices, half_types * 2 * PERIODS), f32), shape((1, PERIODS), f32)),
        in_specs=[SMEM] * 5 + [VMEM] * 6,
        out_specs=(VMEM,) * 2,
        scratch_shapes=work,
    )(patience, productivity, income_levels, income_transition, wage_path, by_row, start, price_row, jac_inverse, supply_row, totals)
    everything = lax.all_to_all(sent, EVERY, split_axis=0, concat_axis=0, tiled=True)
    price_path, market_gap, type_paths = pl.pallas_call(
        functools.partial(last_kernel, half_types=half_types, all_types=all_types),
        name="last_update",
        out_shape=(shape((1, PERIODS), f32), shape((1, PERIODS), f32), shape((local_types, 2, PERIODS), f32)),
        in_specs=[SMEM] + [VMEM] * 5,
        out_specs=(VMEM,) * 3,
    )(assignment, price_row, jac_inverse, supply_row, first_gap, everything)
    return price_path.reshape(PERIODS), market_gap.reshape(PERIODS), type_paths


def solution(mesh):
    torus = Mesh(
        mesh.devices.reshape(4, 8, 4, mesh.shape["tm"]), ("types_0", "types_1", "types_2", "tm")
    )
    in_specs = (
        P(TYPES, "tm", None, None),
        P(TYPES),
        P(TYPES, None, None),
        P(TYPES),
        P(TYPES),
        P(),
        P(),
        P(),
        P(),
        P(),
        P(),
        P(),
    )
    out_specs = (P(), P(), P(TYPES, None, None))
    return jax.shard_map(body, mesh=torus, in_specs=in_specs, out_specs=out_specs, check_vma=False)
```

```python
import functools

import jax
import jax.numpy as jnp
from jax import lax
from jax.experimental import pallas as pl
from jax.experimental.pallas import tpu as pltpu
from jax.sharding import Mesh
from jax.sharding import PartitionSpec as P

ASSETS = 512
INCOME = 7
BLOCK = 128
REACH = 8
PERIODS = 8
HALF = PERIODS // 2
BLOCKS = ASSETS // BLOCK
ROWS = 16
TYPES = ("types_0", "types_1", "types_2")
EVERY = ("types_0", "types_1", "types_2", "tm")

grid_top = 40.0
grid_scale = grid_top / (ASSETS - 1) ** 2
rate_floor = 0.005
rate_span = 0.03

VMEM = pl.BlockSpec(memory_space=pltpu.VMEM)
SMEM = pl.BlockSpec(memory_space=pltpu.SMEM)


def near(array):
    return pltpu.with_memory_space_constraint(array, pltpu.VMEM)


def iota(dim, shape=(ROWS, BLOCK)):
    return lax.broadcasted_iota(jnp.int32, shape, dim)


def by_type(scalars):
    kind = iota(0) // BLOCKS
    value = jnp.full((ROWS, BLOCK), scalars[-1], jnp.float32)
    for k in range(len(scalars) - 2, -1, -1):
        value = jnp.where(kind == k, scalars[k], value)
    return value


def diagonal():
    return iota(0, (PERIODS, PERIODS)) == iota(1, (PERIODS, PERIODS))


def gap_row(totals_row, supply_row, all_types):
    return totals_row * (1.0 / all_types) - supply_row


def price_column(price_row, jac, gaps):
    wide = jnp.where(diagonal(), jnp.broadcast_to(price_row, (PERIODS, PERIODS)), 0.0)
    for gap in gaps:
        wide = wide - jac * gap
    return jnp.sum(wide, axis=1, keepdims=True)


def set_rates(price, rates):
    rate = rate_floor + rate_span / (1.0 + jnp.exp(-price))
    rate = jnp.broadcast_to(rate, (PERIODS, BLOCK))
    rates[0] = rate
    rates[1] = 1.0 / (1.0 + rate)


def solve(core, half_types, patience, productivity, levels, transition, wage, brackets, start, rates, weights, savings, series, full):
    lane, row = iota(1), iota(0)
    point = (row % BLOCKS) * BLOCK + lane
    first = (row % BLOCKS) * BLOCK
    grid = point.astype(jnp.float32)
    grid = grid_scale * grid * grid
    types = [core * half_types + k for k in range(half_types)]
    beta = by_type([patience[k] for k in types])
    skill = by_type([productivity[k] for k in types])
    mixing = [[transition[e, f] for f in range(INCOME)] for e in range(INCOME)]
    pay = [levels[e] for e in range(INCOME)]

    def rate_at(t):
        rate = jnp.broadcast_to(rates[0, pl.ds(t, 1), :], (ROWS, BLOCK))
        inverse = jnp.broadcast_to(rates[1, pl.ds(t, 1), :], (ROWS, BLOCK))
        return rate, inverse

    last, _ = rate_at(PERIODS - 1)
    values = tuple((1.0 + last) / (last * grid + (wage[PERIODS - 1] * pay[e]) * skill) for e in range(INCOME))

    def backward(step, values):
        t = PERIODS - 1 - step
        rate, inverse = rate_at(t)
        budget = (1.0 + rate) * grid
        fresh = []
        for e in range(INCOME):
            mixed = mixing[e][0] * values[0]
            for f in range(1, INCOME):
                mixed = mixed + mixing[e][f] * values[f]
            income = (wage[t] * pay[e]) * skill
            edge = (1.0 / (beta * mixed) + grid - income) * inverse
            above = pltpu.roll(edge, 1, 0)
            bracket = brackets[t, e]
            spot, after = bracket & (BLOCK - 1), (bracket + 1) & (BLOCK - 1)
            lower = jnp.where(
                bracket >= first,
                jnp.take_along_axis(edge, spot, axis=1),
                jnp.take_along_axis(above, spot, axis=1),
            )
            upper = jnp.where(
                bracket + 1 >= first,
                jnp.take_along_axis(edge, after, axis=1),
                jnp.take_along_axis(above, after, axis=1),
            )
            place = bracket.astype(jnp.float32)
            low = grid_scale * place * place
            width = grid_scale * (2.0 * place + 1.0)
            spacing = jnp.maximum(upper - lower, width * inverse)
            weight = jnp.clip((grid - lower) / spacing, 0.0, 1.0)
            saved = low + weight * width
            weights[t, e] = weight
            savings[t, e] = saved
            fresh.append((1.0 + rate) / (budget + income - saved))
        return tuple(fresh)

    lax.fori_loop(0, PERIODS, backward, values)

    def sums(t, masses):
        rate, _ = rate_at(t)
        budget = (1.0 + rate) * grid
        assets = jnp.zeros((ROWS, BLOCK), jnp.float32)
        spent = jnp.zeros((ROWS, BLOCK), jnp.float32)
        for e in range(INCOME):
            saved = savings[t, e]
            assets = assets + masses[e] * saved
            if full:
                spent = spent + masses[e] * (budget + (wage[t] * pay[e]) * skill - saved)
        series[0, t] = assets
        if full:
            series[1, t] = spent

    def forward(t, masses):
        sums(t, masses)
        arrived = []
        for e in range(INCOME):
            weight = weights[t, e]
            rising = weight * masses[e]
            staying = (1.0 - weight) * masses[e]
            drop = point - brackets[t, e]
            hit = [drop == s for s in range(REACH + 2)]
            here = jnp.where(hit[0], staying, jnp.where(hit[1], rising, 0.0))
            here = here + pltpu.roll(jnp.where(hit[0], rising, 0.0), 1, 1)
            crossed = jnp.zeros((ROWS, BLOCK), jnp.float32)
            for s in range(1, REACH + 2):
                moved = jnp.where(hit[s], staying, jnp.where(hit[s + 1], rising, 0.0) if s <= REACH else 0.0)
                moved = pltpu.roll(moved, BLOCK - s, 1)
                inside = lane < BLOCK - s
                here = here + jnp.where(inside, moved, 0.0)
                crossed = crossed + jnp.where(inside, 0.0, moved)
            arrived.append(here + pltpu.roll(crossed, ROWS - 1, 0))
        fresh = []
        for f in range(INCOME):
            mixed = mixing[0][f] * arrived[0]
            for e in range(1, INCOME):
                mixed = mixed + mixing[e][f] * arrived[e]
            fresh.append(mixed)
        return tuple(fresh)

    masses = tuple(start[e] for e in range(INCOME))
    masses = lax.fori_loop(0, PERIODS - 1, forward, masses)
    sums(PERIODS - 1, masses)


def lane_sums(arrays):
    lane = iota(1)
    held = jnp.zeros((ROWS, BLOCK), jnp.float32)
    for q, array in enumerate(arrays):
        held = jnp.where(lane == q, jnp.sum(array, axis=1, keepdims=True), held)
    return held


def first_kernel(
    blocks, patience, productivity, levels, transition, wage, mine, theirs, mass, price,
    out, brackets, start, rates, weights, savings, series,
):
    half_types = mine.shape[1]
    core = lax.axis_index("tm")
    for k in range(half_types):
        alive = blocks[core * half_types + k]
        for e in range(INCOME):
            for b in range(BLOCKS):
                line = pl.ds(k * BLOCKS + b, 1)
                part = pl.ds(b * BLOCK, BLOCK)
                live = (b < alive).astype(jnp.float32)
                start[e, line, :] = mass[core * half_types + k, pl.ds(e, 1), part] * live
                for t in range(HALF):
                    brackets[core * HALF + t, e, line, :] = mine[core, k, e, pl.ds(t, 1), part]
                    brackets[(1 - core) * HALF + t, e, line, :] = theirs[core, k, e, pl.ds(t, 1), part]
    spare = ROWS - half_types * BLOCKS
    for e in range(INCOME):
        start[e, ROWS - spare :, :] = jnp.zeros((spare, BLOCK), jnp.float32)
        for t in range(PERIODS):
            brackets[t, e, ROWS - spare :, :] = brackets[t, e, ROWS - 2 * spare : ROWS - spare, :]
    set_rates(price_column(price[...], None, ()), rates)
    solve(core, half_types, patience, productivity, levels, transition, wage, brackets, start, rates, weights, savings, series, False)
    held = lane_sums([series[0, t] for t in range(PERIODS)])
    total = jnp.sum(held, axis=0, keepdims=True)[:, :PERIODS]
    out[...] = total


def second_kernel(
    patience, productivity, levels, transition, wage, brackets, start, price, jac, supply, totals,
    out, gap_out, rates, weights, savings, series,
    *, half_types, all_types,
):
    core = lax.axis_index("tm")
    total = jnp.sum(totals[...], axis=0, keepdims=True)
    gap = gap_row(total, supply[...], all_types)
    gap_out[...] = gap
    set_rates(price_column(price[...], jac[...], (gap,)), rates)
    solve(core, half_types, patience, productivity, levels, transition, wage, brackets, start, rates, weights, savings, series, True)
    held = lane_sums([series[c, t] for c in range(2) for t in range(PERIODS)])
    for k in range(half_types):
        line = jnp.sum(held[k * BLOCKS : (k + 1) * BLOCKS], axis=0, keepdims=True)
        width = 2 * PERIODS
        out[:, k * width : (k + 1) * width] = line[:, :width]


def last_kernel(assignment, price, jac, supply, first_gap, everything, price_out, gap_out, paths_out, *, half_types, all_types):
    here = lax.axis_index(TYPES)
    width = 2 * PERIODS
    total = jnp.sum(everything[...], axis=0, keepdims=True)
    assets = total[:, :PERIODS]
    for k in range(1, half_types):
        assets = assets + total[:, k * width : k * width + PERIODS]
    gap = gap_row(assets, supply[...], all_types)
    gap_out[...] = gap
    column = price_column(price[...], jac[...], (first_gap[...], gap))
    price_out[...] = jnp.sum(jnp.where(diagonal(), column, 0.0), axis=0, keepdims=True)
    slots = paths_out.shape[0]
    for s in range(slots):
        wanted = assignment[here * slots + s]
        line = everything[pl.ds(wanted // half_types, 1), :]
        kind = wanted % half_types
        found = line[:, :width]
        for k in range(1, half_types):
            found = jnp.where(kind == k, line[:, k * width : (k + 1) * width], found)
        for c in range(2):
            paths_out[s, pl.ds(c, 1), :] = found[:, c * PERIODS : (c + 1) * PERIODS]


def body(
    brackets,
    active_blocks,
    initial_mass,
    patience,
    productivity,
    income_levels,
    income_transition,
    wage_path,
    bond_supply,
    price_guess,
    jac_inverse,
    assignment,
):
    local_types = patience.shape[0]
    all_types = local_types * lax.axis_size(TYPES)
    cores = lax.axis_size("tm")
    devices = lax.axis_size(EVERY)
    half_types = local_types // cores
    f32, i32 = jnp.float32, jnp.int32
    shape = jax.ShapeDtypeStruct
    by_income = jnp.transpose(brackets, (0, 2, 1, 3)).reshape(cores, half_types, INCOME, HALF, ASSETS)
    theirs = lax.ppermute(by_income, "tm", [(c, cores - 1 - c) for c in range(cores)])
    theirs = near(theirs)

    def exchanged(line):
        copies = jnp.broadcast_to(line[None], (devices, 1, line.shape[1]))
        return lax.all_to_all(copies, EVERY, split_axis=0, concat_axis=0, tiled=True).reshape(devices, -1)

    price_row = price_guess.reshape(1, PERIODS)
    supply_row = bond_supply.reshape(1, PERIODS)
    work = [
        pltpu.VMEM((2, PERIODS, BLOCK), f32),
        pltpu.VMEM((PERIODS, INCOME, ROWS, BLOCK), f32),
        pltpu.VMEM((PERIODS, INCOME, ROWS, BLOCK), f32),
        pltpu.VMEM((2, PERIODS, ROWS, BLOCK), f32),
    ]
    sent, by_row, start = pl.pallas_call(
        first_kernel,
        name="first_round",
        out_shape=(
            pltpu.VMEM((1, PERIODS), f32),
            pltpu.VMEM((PERIODS, INCOME, ROWS, BLOCK), i32),
            pltpu.VMEM((INCOME, ROWS, BLOCK), f32),
        ),
        in_specs=[SMEM] * 6 + [VMEM] * 4,
        out_specs=(VMEM,) * 3,
        scratch_shapes=work,
    )(active_blocks, patience, productivity, income_levels, income_transition, wage_path, by_income, theirs, initial_mass, price_row)
    totals = near(exchanged(sent))
    sent, first_gap = pl.pallas_call(
        functools.partial(second_kernel, half_types=half_types, all_types=all_types),
        name="second_round",
        out_shape=(pltpu.VMEM((1, half_types * 2 * PERIODS), f32), pltpu.VMEM((1, PERIODS), f32)),
        in_specs=[SMEM] * 5 + [VMEM] * 6,
        out_specs=(VMEM,) * 2,
        scratch_shapes=work,
    )(patience, productivity, income_levels, income_transition, wage_path, near(by_row), near(start), price_row, jac_inverse, supply_row, totals)
    everything = near(exchanged(sent))
    price_path, market_gap, type_paths = pl.pallas_call(
        functools.partial(last_kernel, half_types=half_types, all_types=all_types),
        name="last_update",
        out_shape=(shape((1, PERIODS), f32), shape((1, PERIODS), f32), shape((local_types, 2, PERIODS), f32)),
        in_specs=[SMEM] + [VMEM] * 5,
        out_specs=(VMEM,) * 3,
    )(assignment, price_row, jac_inverse, supply_row, near(first_gap), everything)
    return price_path.reshape(PERIODS), market_gap.reshape(PERIODS), type_paths


def solution(mesh):
    torus = Mesh(
        mesh.devices.reshape(4, 8, 4, mesh.shape["tm"]), ("types_0", "types_1", "types_2", "tm")
    )
    in_specs = (
        P(TYPES, "tm", None, None),
        P(TYPES),
        P(TYPES, None, None),
        P(TYPES),
        P(TYPES),
        P(),
        P(),
        P(),
        P(),
        P(),
        P(),
        P(),
    )
    out_specs = (P(), P(), P(TYPES, None, None))
    return jax.shard_map(body, mesh=torus, in_specs=in_specs, out_specs=out_specs, check_vma=False)
```

```python
import functools

import jax
import jax.numpy as jnp
from jax import lax
from jax.experimental import pallas as pl
from jax.experimental.pallas import tpu as pltpu
from jax.sharding import Mesh
from jax.sharding import PartitionSpec as P

ASSETS = 512
INCOME = 7
BLOCK = 128
REACH = 8
PERIODS = 8
HALF = PERIODS // 2
BLOCKS = ASSETS // BLOCK
TILE = 8
SHARE = 3 * BLOCKS
LINES = INCOME * SHARE
CHUNKS = -(-LINES // TILE)
ROWS = CHUNKS * TILE
DEEP = ROWS + 2 * TILE
WIDE = 2 * TILE
FRAME = 2 * SHARE
WAGE = 56
TYPES = ("types_0", "types_1", "types_2")
EVERY = ("types_0", "types_1", "types_2", "tm")

grid_top = 40.0
grid_scale = grid_top / (ASSETS - 1) ** 2
rate_floor = 0.005
rate_span = 0.03

VMEM = pl.BlockSpec(memory_space=pltpu.VMEM)
SMEM = pl.BlockSpec(memory_space=pltpu.SMEM)


def near(array):
    return pltpu.with_memory_space_constraint(array, pltpu.VMEM)


def iota(dim, shape=(TILE, BLOCK)):
    return lax.broadcasted_iota(jnp.int32, shape, dim)


def rows_of(chunk):
    return pl.ds(chunk * TILE, TILE)


def splat(row, rows=TILE):
    return jnp.broadcast_to(row, (rows, BLOCK))


def diagonal():
    return iota(0, (PERIODS, PERIODS)) == iota(1, (PERIODS, PERIODS))


def gap_row(totals_row, supply_row, all_types):
    return totals_row * (1.0 / all_types) - supply_row


def price_column(price_row, jac, gaps):
    wide = jnp.where(diagonal(), jnp.broadcast_to(price_row, (PERIODS, PERIODS)), 0.0)
    for gap in gaps:
        wide = wide - jac * gap
    return jnp.sum(wide, axis=1, keepdims=True)


def set_rates(price, rates):
    rate = rate_floor + rate_span / (1.0 + jnp.exp(-price))
    rate = jnp.broadcast_to(rate, (PERIODS, BLOCK))
    rates[0] = rate
    rates[1] = 1.0 / (1.0 + rate)


def pattern():
    first = (iota(0) % BLOCKS) * BLOCK
    point = first + iota(1)
    place = point.astype(jnp.float32)
    return point, first, grid_scale * place * place


def mix(source, target, consts, offset, transposed):
    states = [source(e) for e in range(INCOME)]
    for e in range(INCOME):
        total = None
        for f in range(INCOME):
            at = f * INCOME + e if transposed else e * INCOME + f
            term = splat(consts[pl.ds(at, 1), :], WIDE) * states[f]
            total = term if total is None else total + term
        target[pl.ds(offset + e * SHARE, WIDE), :] = total


def solve(consts, beta, pay, brackets, start, rates, weights, savings, values, edges, masses, crossings, series, full):
    point, first, grid = pattern()
    lane = iota(1)

    def rate_at(t):
        return splat(rates[0, pl.ds(t, 1), :]), splat(rates[1, pl.ds(t, 1), :])

    def wage_at(t):
        return splat(consts[pl.ds(WAGE + t, 1), :])

    last, _ = rate_at(PERIODS - 1)
    wage = wage_at(PERIODS - 1)
    for c in range(CHUNKS):
        values[rows_of(c), :] = (1.0 + last) / (last * grid + wage * pay[rows_of(c), :])

    def backward(step, carried):
        t = PERIODS - 1 - step
        rate, inverse = rate_at(t)
        wage = wage_at(t)
        budget = (1.0 + rate) * grid
        mix(lambda e: values[pl.ds(e * SHARE, WIDE), :], edges, consts, TILE, False)
        for c in range(CHUNKS):
            line = pl.ds(TILE + c * TILE, TILE)
            income = wage * pay[rows_of(c), :]
            edges[line, :] = (1.0 / (beta[rows_of(c), :] * edges[line, :]) + grid - income) * inverse
        for c in range(CHUNKS):
            income = wage * pay[rows_of(c), :]
            edge = edges[pl.ds(TILE + c * TILE, TILE), :]
            above = edges[pl.ds(TILE + c * TILE - 1, TILE), :]
            bracket = brackets[t, rows_of(c), :]
            spot, after = bracket & (BLOCK - 1), (bracket + 1) & (BLOCK - 1)
            lower = jnp.where(
                bracket >= first,
                jnp.take_along_axis(edge, spot, axis=1),
                jnp.take_along_axis(above, spot, axis=1),
            )
            upper = jnp.where(
                bracket + 1 >= first,
                jnp.take_along_axis(edge, after, axis=1),
                jnp.take_along_axis(above, after, axis=1),
            )
            place = bracket.astype(jnp.float32)
            low = grid_scale * place * place
            width = grid_scale * (2.0 * place + 1.0)
            spacing = jnp.maximum(upper - lower, width * inverse)
            weight = jnp.clip((grid - lower) / spacing, 0.0, 1.0)
            saved = low + weight * width
            weights[t, rows_of(c), :] = weight
            savings[t, rows_of(c), :] = saved
            values[rows_of(c), :] = (1.0 + rate) / (budget + income - saved)
        return carried

    lax.fori_loop(0, PERIODS, backward, 0)
    for c in range(CHUNKS):
        masses[rows_of(c), :] = start[rows_of(c), :]

    def sums(t):
        rate, _ = rate_at(t)
        wage = wage_at(t)
        budget = (1.0 + rate) * grid
        parts = FRAME // TILE
        assets, spent = [None] * parts, [None] * parts
        for c in range(CHUNKS):
            mass, saved = masses[rows_of(c), :], savings[t, rows_of(c), :]
            terms = [mass * saved]
            if full:
                terms.append(mass * (budget + wage * pay[rows_of(c), :] - saved))
            if (c + 1) * TILE > LINES:
                terms = [jnp.where(iota(0) < LINES - c * TILE, term, 0.0) for term in terms]
            for held, term in zip((assets, spent), terms):
                held[c % parts] = term if held[c % parts] is None else held[c % parts] + term
        for q, held in enumerate((assets, spent) if full else (assets,)):
            for part in range(parts):
                series[q, t, pl.ds(part * TILE, TILE), :] = held[part]

    def forward(t, carried):
        sums(t)
        for c in range(CHUNKS):
            mass, weight = masses[rows_of(c), :], weights[t, rows_of(c), :]
            rising = weight * mass
            staying = (1.0 - weight) * mass
            drop = point - brackets[t, rows_of(c), :]
            hit = [drop == s for s in range(REACH + 2)]
            here = jnp.where(hit[0], staying, jnp.where(hit[1], rising, 0.0))
            here = here + pltpu.roll(jnp.where(hit[0], rising, 0.0), 1, 1)
            crossed = jnp.zeros((TILE, BLOCK), jnp.float32)
            for s in range(1, REACH + 2):
                moved = jnp.where(hit[s], staying, jnp.where(hit[s + 1], rising, 0.0) if s <= REACH else 0.0)
                moved = pltpu.roll(moved, BLOCK - s, 1)
                inside = lane < BLOCK - s
                here = here + jnp.where(inside, moved, 0.0)
                crossed = crossed + jnp.where(inside, 0.0, moved)
            edges[rows_of(c), :] = here
            crossings[rows_of(c), :] = crossed

        def arrived(e):
            return edges[pl.ds(e * SHARE, WIDE), :] + crossings[pl.ds(e * SHARE + 1, WIDE), :]

        mix(arrived, masses, consts, 0, True)
        return carried

    lax.fori_loop(0, PERIODS - 1, forward, 0)
    sums(PERIODS - 1)


def start_kernel(
    blocks, patience, productivity, levels, transition, wage, assignment, mine, mass, price_in, jac_in, supply_in,
    own, start, consts, beta, pay, wanted, price, jac, supply,
):
    price[...], jac[...], supply[...] = price_in[...], jac_in[...], supply_in[...]
    half_types = mine.shape[1]
    core = lax.axis_index("tm")
    here = lax.axis_index(TYPES)
    for e in range(INCOME):
        for f in range(INCOME):
            consts[e * INCOME + f : e * INCOME + f + 1, :] = jnp.full((1, BLOCK), transition[e, f], jnp.float32)
    for t in range(PERIODS):
        consts[WAGE + t : WAGE + t + 1, :] = jnp.full((1, BLOCK), wage[t], jnp.float32)
    for s in range(TILE):
        slot = here * 2 * half_types + min(s, 2 * half_types - 1)
        wanted[s : s + 1, :] = jnp.full((1, BLOCK), assignment[slot], jnp.int32)
    for k in range(half_types):
        alive = blocks[core * half_types + k]
        patient, skill = patience[core * half_types + k], productivity[core * half_types + k]
        for e in range(INCOME):
            top = e * SHARE + k * BLOCKS
            beta[top : top + BLOCKS, :] = jnp.full((BLOCKS, BLOCK), patient, jnp.float32)
            pay[top : top + BLOCKS, :] = jnp.full((BLOCKS, BLOCK), skill * levels[e], jnp.float32)
            for b in range(BLOCKS):
                line, part = pl.ds(top + b, 1), pl.ds(b * BLOCK, BLOCK)
                live = (b < alive).astype(jnp.float32)
                start[line, :] = mass[core * half_types + k, pl.ds(e, 1), part] * live
                for t in range(HALF):
                    own[t, line, :] = mine[core, k, e, pl.ds(t, 1), part]
    spare = ROWS - LINES
    beta[LINES:, :] = jnp.ones((spare, BLOCK), jnp.float32)
    pay[LINES:, :] = jnp.ones((spare, BLOCK), jnp.float32)
    start[LINES:, :] = jnp.zeros((spare, BLOCK), jnp.float32)
    for t in range(HALF):
        own[t, LINES:, :] = jnp.zeros((spare, BLOCK), jnp.int32)


def first_kernel(
    own, theirs, start, consts, beta, pay, price,
    out, brackets, rates, weights, savings, values, edges, masses, crossings, series,
):
    half_types = theirs.shape[1]
    core = lax.axis_index("tm")
    for t in range(HALF):
        brackets[core * HALF + t] = own[t]
        brackets[(1 - core) * HALF + t, LINES:, :] = jnp.zeros((ROWS - LINES, BLOCK), jnp.int32)
    for k in range(half_types):
        for e in range(INCOME):
            for b in range(BLOCKS):
                line, part = pl.ds(e * SHARE + k * BLOCKS + b, 1), pl.ds(b * BLOCK, BLOCK)
                for t in range(HALF):
                    brackets[(1 - core) * HALF + t, line, :] = theirs[core, k, e, pl.ds(t, 1), part]
    set_rates(price_column(price[...], None, ()), rates)
    solve(consts, beta, pay, brackets, start, rates, weights, savings, values, edges, masses, crossings, series, False)
    lane = iota(1)
    held = jnp.zeros((TILE, BLOCK), jnp.float32)
    for t in range(PERIODS):
        total = series[0, t, :TILE, :]
        for part in range(1, FRAME // TILE):
            total = total + series[0, t, part * TILE : (part + 1) * TILE, :]
        held = jnp.where(lane == t, jnp.sum(total, axis=1, keepdims=True), held)
    out[...] = jnp.sum(held, axis=0, keepdims=True)[:, :PERIODS]


def second_kernel(
    brackets, start, consts, beta, pay, price, jac, supply, totals,
    out, gap_out, rates, weights, savings, values, edges, masses, crossings, series,
    *, half_types, all_types,
):
    total = jnp.sum(totals[...], axis=0, keepdims=True)
    gap = gap_row(total, supply[...], all_types)
    gap_out[...] = gap
    set_rates(price_column(price[...], jac[...], (gap,)), rates)
    solve(consts, beta, pay, brackets, start, rates, weights, savings, values, edges, masses, crossings, series, True)
    lane = iota(1, (SHARE, BLOCK))
    held = jnp.zeros((SHARE, BLOCK), jnp.float32)
    width = 2 * PERIODS
    for q in range(width):
        both = series[q // PERIODS, q % PERIODS, :SHARE, :] + series[q // PERIODS, q % PERIODS, SHARE:, :]
        held = jnp.where(lane == q, jnp.sum(both, axis=1, keepdims=True), held)
    for k in range(half_types):
        line = jnp.sum(held[k * BLOCKS : (k + 1) * BLOCKS], axis=0, keepdims=True)
        out[:, k * width : (k + 1) * width] = line[:, :width]


def last_kernel(wanted, price, jac, supply, first_gap, everything, price_out, gap_out, paths_out, *, half_types, all_types):
    width = 2 * PERIODS
    rows = everything.shape[0]
    total = jnp.sum(everything[...], axis=0, keepdims=True)
    assets = total[:, :PERIODS]
    for k in range(1, half_types):
        assets = assets + total[:, k * width : k * width + PERIODS]
    gap = gap_row(assets, supply[...], all_types)
    gap_out[...] = gap
    column = price_column(price[...], jac[...], (first_gap[...], gap))
    price_out[...] = jnp.sum(jnp.where(diagonal(), column, 0.0), axis=0, keepdims=True)
    span = half_types * width
    owner = iota(0, (rows, span)) * half_types + iota(1, (rows, span)) // width
    for s in range(paths_out.shape[0]):
        picked = jnp.where(owner == wanted[pl.ds(s, 1), :span], everything[...], 0.0)
        line = jnp.sum(picked, axis=0, keepdims=True)
        found = line[:, :width]
        for k in range(1, half_types):
            found = found + line[:, k * width : (k + 1) * width]
        for c in range(2):
            paths_out[s, pl.ds(c, 1), :] = found[:, c * PERIODS : (c + 1) * PERIODS]


def body(
    brackets,
    active_blocks,
    initial_mass,
    patience,
    productivity,
    income_levels,
    income_transition,
    wage_path,
    bond_supply,
    price_guess,
    jac_inverse,
    assignment,
):
    local_types = patience.shape[0]
    all_types = local_types * lax.axis_size(TYPES)
    cores = lax.axis_size("tm")
    devices = lax.axis_size(EVERY)
    half_types = local_types // cores
    f32, i32 = jnp.float32, jnp.int32
    by_income = jnp.transpose(brackets, (0, 2, 1, 3)).reshape(cores, half_types, INCOME, HALF, ASSETS)
    theirs = near(lax.ppermute(by_income, "tm", [(c, cores - 1 - c) for c in range(cores)]))

    def exchanged(line):
        copies = jnp.broadcast_to(line[None], (devices, 1, line.shape[1]))
        return near(lax.all_to_all(copies, EVERY, split_axis=0, concat_axis=0, tiled=True).reshape(devices, -1))

    work = [
        pltpu.VMEM((2, PERIODS, BLOCK), f32),
        pltpu.VMEM((PERIODS, ROWS, BLOCK), f32),
        pltpu.VMEM((PERIODS, ROWS, BLOCK), f32),
        pltpu.VMEM((DEEP, BLOCK), f32),
        pltpu.VMEM((DEEP, BLOCK), f32),
        pltpu.VMEM((DEEP, BLOCK), f32),
        pltpu.VMEM((DEEP, BLOCK), f32),
        pltpu.VMEM((2, PERIODS, FRAME, BLOCK), f32),
    ]
    own, *shared, wanted, price_row, jac, supply_row = pl.pallas_call(
        start_kernel,
        name="start",
        out_shape=(
            pltpu.VMEM((HALF, ROWS, BLOCK), i32),
            pltpu.VMEM((ROWS, BLOCK), f32),
            pltpu.VMEM((WAGE + PERIODS, BLOCK), f32),
            pltpu.VMEM((ROWS, BLOCK), f32),
            pltpu.VMEM((ROWS, BLOCK), f32),
            pltpu.VMEM((TILE, BLOCK), i32),
            pltpu.VMEM((1, PERIODS), f32),
            pltpu.VMEM((PERIODS, PERIODS), f32),
            pltpu.VMEM((1, PERIODS), f32),
        ),
        in_specs=[SMEM] * 7 + [VMEM] * 5,
        out_specs=(VMEM,) * 9,
        cost_estimate=pl.CostEstimate(flops=100000, bytes_accessed=2000000, transcendentals=0),
    )(
        active_blocks, patience, productivity, income_levels, income_transition, wage_path, assignment, by_income,
        initial_mass, price_guess.reshape(1, PERIODS), jac_inverse, bond_supply.reshape(1, PERIODS),
    )
    price_row, jac, supply_row = near(price_row), near(jac), near(supply_row)
    shared = [near(array) for array in shared]
    sent, by_row = pl.pallas_call(
        first_kernel,
        name="first_round",
        out_shape=(pltpu.VMEM((1, PERIODS), f32), pltpu.VMEM((PERIODS, ROWS, BLOCK), i32)),
        in_specs=[VMEM] * 7,
        out_specs=(VMEM,) * 2,
        scratch_shapes=work,
    )(near(own), theirs, *shared, price_row)
    totals = exchanged(sent)
    sent, first_gap = pl.pallas_call(
        functools.partial(second_kernel, half_types=half_types, all_types=all_types),
        name="second_round",
        out_shape=(pltpu.VMEM((1, half_types * 2 * PERIODS), f32), pltpu.VMEM((1, PERIODS), f32)),
        in_specs=[VMEM] * 9,
        out_specs=(VMEM,) * 2,
        scratch_shapes=work,
    )(near(by_row), *shared, price_row, jac, supply_row, totals)
    everything = exchanged(sent)
    price_path, market_gap, type_paths = pl.pallas_call(
        functools.partial(last_kernel, half_types=half_types, all_types=all_types),
        name="last_update",
        out_shape=(
            jax.ShapeDtypeStruct((1, PERIODS), f32),
            jax.ShapeDtypeStruct((1, PERIODS), f32),
            jax.ShapeDtypeStruct((local_types, 2, PERIODS), f32),
        ),
        in_specs=[VMEM] * 6,
        out_specs=(VMEM,) * 3,
    )(near(wanted), price_row, jac, supply_row, near(first_gap), everything)
    return price_path.reshape(PERIODS), market_gap.reshape(PERIODS), type_paths


def solution(mesh):
    torus = Mesh(
        mesh.devices.reshape(4, 8, 4, mesh.shape["tm"]), ("types_0", "types_1", "types_2", "tm")
    )
    in_specs = (
        P(TYPES, "tm", None, None),
        P(TYPES),
        P(TYPES, None, None),
        P(TYPES),
        P(TYPES),
        P(),
        P(),
        P(),
        P(),
        P(),
        P(),
        P(),
    )
    out_specs = (P(), P(), P(TYPES, None, None))
    return jax.shard_map(body, mesh=torus, in_specs=in_specs, out_specs=out_specs, check_vma=False)
```

```python
import functools

import jax
import jax.numpy as jnp
from jax import lax
from jax.experimental import pallas as pl
from jax.experimental.pallas import tpu as pltpu
from jax.sharding import Mesh
from jax.sharding import PartitionSpec as P

ASSETS = 512
INCOME = 7
BLOCK = 128
REACH = 8
PERIODS = 8
HALF = PERIODS // 2
BLOCKS = ASSETS // BLOCK
TILE = 8
SHARE = 3 * BLOCKS
LINES = INCOME * SHARE
CHUNKS = -(-LINES // TILE)
ROWS = CHUNKS * TILE
DEEP = ROWS + 2 * TILE
WIDE = 2 * TILE
FRAME = 2 * SHARE
WAGE = 56
TYPES = ("types_0", "types_1", "types_2")
EVERY = ("types_0", "types_1", "types_2", "tm")

grid_top = 40.0
grid_scale = grid_top / (ASSETS - 1) ** 2
rate_floor = 0.005
rate_span = 0.03

VMEM = pl.BlockSpec(memory_space=pltpu.VMEM)
SMEM = pl.BlockSpec(memory_space=pltpu.SMEM)


def near(array):
    return pltpu.with_memory_space_constraint(array, pltpu.VMEM)


def iota(dim, shape=(TILE, BLOCK)):
    return lax.broadcasted_iota(jnp.int32, shape, dim)


def rows_of(chunk):
    return pl.ds(chunk * TILE, TILE)


def splat(row, rows=TILE):
    return jnp.broadcast_to(row, (rows, BLOCK))


def diagonal():
    return iota(0, (PERIODS, PERIODS)) == iota(1, (PERIODS, PERIODS))


def gap_row(totals_row, supply_row, all_types):
    return totals_row * (1.0 / all_types) - supply_row


def price_column(price_row, jac, gaps):
    wide = jnp.where(diagonal(), jnp.broadcast_to(price_row, (PERIODS, PERIODS)), 0.0)
    for gap in gaps:
        wide = wide - jac * gap
    return jnp.sum(wide, axis=1, keepdims=True)


def set_rates(price, rates):
    rate = rate_floor + rate_span / (1.0 + jnp.exp(-price))
    rate = jnp.broadcast_to(rate, (PERIODS, BLOCK))
    rates[0] = rate
    rates[1] = 1.0 / (1.0 + rate)


def pattern():
    first = (iota(0) % BLOCKS) * BLOCK
    point = first + iota(1)
    place = point.astype(jnp.float32)
    return point, first, grid_scale * place * place


def mix(source, target, consts, offset, transposed):
    states = [source(e) for e in range(INCOME)]
    for e in range(INCOME):
        terms = []
        for f in range(INCOME):
            at = f * INCOME + e if transposed else e * INCOME + f
            terms.append(splat(consts[pl.ds(at, 1), :], WIDE) * states[f])
        while len(terms) > 1:
            terms = [sum(terms[i + 1 : i + 2], terms[i]) for i in range(0, len(terms), 2)]
        target[pl.ds(offset + e * SHARE, WIDE), :] = terms[0]


def solve(consts, beta, pay, brackets, start, rates, weights, savings, values, edges, masses, crossings, series, full):
    point, first, grid = pattern()
    lane = iota(1)

    def rate_at(t):
        return splat(rates[0, pl.ds(t, 1), :]), splat(rates[1, pl.ds(t, 1), :])

    def wage_at(t):
        return splat(consts[pl.ds(WAGE + t, 1), :])

    last, _ = rate_at(PERIODS - 1)
    wage = wage_at(PERIODS - 1)
    for c in range(CHUNKS):
        values[rows_of(c), :] = (1.0 + last) / (last * grid + wage * pay[rows_of(c), :])

    def backward(step, carried):
        t = PERIODS - 1 - step
        rate, inverse = rate_at(t)
        wage = wage_at(t)
        budget = (1.0 + rate) * grid
        mix(lambda e: values[pl.ds(e * SHARE, WIDE), :], edges, consts, TILE, False)
        for c in range(CHUNKS):
            line = pl.ds(TILE + c * TILE, TILE)
            income = wage * pay[rows_of(c), :]
            edges[line, :] = (1.0 / (beta[rows_of(c), :] * edges[line, :]) + grid - income) * inverse
        for c in range(CHUNKS):
            income = wage * pay[rows_of(c), :]
            edge = edges[pl.ds(TILE + c * TILE, TILE), :]
            above = edges[pl.ds(TILE + c * TILE - 1, TILE), :]
            bracket = brackets[t, rows_of(c), :]
            spot, after = bracket & (BLOCK - 1), (bracket + 1) & (BLOCK - 1)
            lower = jnp.where(
                bracket >= first,
                jnp.take_along_axis(edge, spot, axis=1),
                jnp.take_along_axis(above, spot, axis=1),
            )
            upper = jnp.where(
                bracket + 1 >= first,
                jnp.take_along_axis(edge, after, axis=1),
                jnp.take_along_axis(above, after, axis=1),
            )
            place = bracket.astype(jnp.float32)
            low = grid_scale * place * place
            width = grid_scale * (2.0 * place + 1.0)
            spacing = jnp.maximum(upper - lower, width * inverse)
            reached = jnp.clip(grid - lower, 0.0, spacing)
            values[rows_of(c), :] = (1.0 + rate) * spacing / ((budget + income - low) * spacing - reached * width)
            weight = reached / spacing
            weights[t, rows_of(c), :] = weight
            savings[t, rows_of(c), :] = low + weight * width
        return carried

    lax.fori_loop(0, PERIODS, backward, 0, unroll=4)
    for c in range(CHUNKS):
        masses[rows_of(c), :] = start[rows_of(c), :]

    def sums(t):
        rate, _ = rate_at(t)
        wage = wage_at(t)
        budget = (1.0 + rate) * grid
        parts = FRAME // TILE
        assets, spent = [None] * parts, [None] * parts
        for c in range(CHUNKS):
            mass, saved = masses[rows_of(c), :], savings[t, rows_of(c), :]
            terms = [mass * saved]
            if full:
                terms.append(mass * (budget + wage * pay[rows_of(c), :] - saved))
            if (c + 1) * TILE > LINES:
                terms = [jnp.where(iota(0) < LINES - c * TILE, term, 0.0) for term in terms]
            for held, term in zip((assets, spent), terms):
                held[c % parts] = term if held[c % parts] is None else held[c % parts] + term
        for q, held in enumerate((assets, spent) if full else (assets,)):
            for part in range(parts):
                series[q, t, pl.ds(part * TILE, TILE), :] = held[part]

    def forward(t, carried):
        sums(t)
        for c in range(CHUNKS):
            mass, weight = masses[rows_of(c), :], weights[t, rows_of(c), :]
            rising = weight * mass
            staying = (1.0 - weight) * mass
            drop = point - brackets[t, rows_of(c), :]
            hit = [drop == s for s in range(REACH + 2)]
            here = jnp.where(hit[0], staying, jnp.where(hit[1], rising, 0.0))
            here = here + pltpu.roll(jnp.where(hit[0], rising, 0.0), 1, 1)
            parts = []
            for s in range(1, REACH + 2):
                moved = jnp.where(hit[s], staying, jnp.where(hit[s + 1], rising, 0.0) if s <= REACH else 0.0)
                moved = pltpu.roll(moved, BLOCK - s, 1)
                inside = lane < BLOCK - s
                parts.append((jnp.where(inside, moved, 0.0), jnp.where(inside, 0.0, moved)))
            while len(parts) > 1:
                parts = [tuple(sum(z[1:], z[0]) for z in zip(*parts[i : i + 2])) for i in range(0, len(parts), 2)]
            here, crossed = here + parts[0][0], parts[0][1]
            edges[rows_of(c), :] = here
            crossings[rows_of(c), :] = crossed

        def arrived(e):
            return edges[pl.ds(e * SHARE, WIDE), :] + crossings[pl.ds(e * SHARE + 1, WIDE), :]

        mix(arrived, masses, consts, 0, True)
        return carried

    lax.fori_loop(0, PERIODS - 1, forward, 0, unroll=True)
    sums(PERIODS - 1)


def start_kernel(
    blocks, patience, productivity, levels, transition, wage, assignment, mine, mass, price_in, jac_in, supply_in,
    own, start, consts, beta, pay, wanted, price, jac, supply,
):
    price[...], jac[...], supply[...] = price_in[...], jac_in[...], supply_in[...]
    half_types = mine.shape[1]
    core = lax.axis_index("tm")
    here = lax.axis_index(TYPES)
    for e in range(INCOME):
        for f in range(INCOME):
            consts[e * INCOME + f : e * INCOME + f + 1, :] = jnp.full((1, BLOCK), transition[e, f], jnp.float32)
    for t in range(PERIODS):
        consts[WAGE + t : WAGE + t + 1, :] = jnp.full((1, BLOCK), wage[t], jnp.float32)
    for s in range(TILE):
        slot = here * 2 * half_types + min(s, 2 * half_types - 1)
        wanted[s : s + 1, :] = jnp.full((1, BLOCK), assignment[slot], jnp.int32)
    for k in range(half_types):
        alive = blocks[core * half_types + k]
        patient, skill = patience[core * half_types + k], productivity[core * half_types + k]
        for e in range(INCOME):
            top = e * SHARE + k * BLOCKS
            beta[top : top + BLOCKS, :] = jnp.full((BLOCKS, BLOCK), patient, jnp.float32)
            pay[top : top + BLOCKS, :] = jnp.full((BLOCKS, BLOCK), skill * levels[e], jnp.float32)
            for b in range(BLOCKS):
                line, part = pl.ds(top + b, 1), pl.ds(b * BLOCK, BLOCK)
                live = (b < alive).astype(jnp.float32)
                start[line, :] = mass[core * half_types + k, pl.ds(e, 1), part] * live
                for t in range(HALF):
                    own[t, line, :] = mine[core, k, e, pl.ds(t, 1), part]
    spare = ROWS - LINES
    beta[LINES:, :] = jnp.ones((spare, BLOCK), jnp.float32)
    pay[LINES:, :] = jnp.ones((spare, BLOCK), jnp.float32)
    start[LINES:, :] = jnp.zeros((spare, BLOCK), jnp.float32)
    for t in range(HALF):
        own[t, LINES:, :] = jnp.zeros((spare, BLOCK), jnp.int32)


def first_kernel(
    own, theirs, start, consts, beta, pay, price,
    out, brackets, rates, weights, savings, values, edges, masses, crossings, series,
):
    half_types = theirs.shape[1]
    core = lax.axis_index("tm")
    for t in range(HALF):
        brackets[core * HALF + t] = own[t]
        brackets[(1 - core) * HALF + t, LINES:, :] = jnp.zeros((ROWS - LINES, BLOCK), jnp.int32)
    for k in range(half_types):
        for e in range(INCOME):
            for b in range(BLOCKS):
                line, part = pl.ds(e * SHARE + k * BLOCKS + b, 1), pl.ds(b * BLOCK, BLOCK)
                for t in range(HALF):
                    brackets[(1 - core) * HALF + t, line, :] = theirs[core, k, e, pl.ds(t, 1), part]
    set_rates(price_column(price[...], None, ()), rates)
    solve(consts, beta, pay, brackets, start, rates, weights, savings, values, edges, masses, crossings, series, False)
    lane = iota(1)
    held = jnp.zeros((TILE, BLOCK), jnp.float32)
    for t in range(PERIODS):
        total = series[0, t, :TILE, :]
        for part in range(1, FRAME // TILE):
            total = total + series[0, t, part * TILE : (part + 1) * TILE, :]
        held = jnp.where(lane == t, jnp.sum(total, axis=1, keepdims=True), held)
    out[...] = jnp.sum(held, axis=0, keepdims=True)[:, :PERIODS]


def second_kernel(
    brackets, start, consts, beta, pay, price, jac, supply, totals,
    out, gap_out, rates, weights, savings, values, edges, masses, crossings, series,
    *, half_types, all_types,
):
    total = jnp.sum(totals[...], axis=0, keepdims=True)
    gap = gap_row(total, supply[...], all_types)
    gap_out[...] = gap
    set_rates(price_column(price[...], jac[...], (gap,)), rates)
    solve(consts, beta, pay, brackets, start, rates, weights, savings, values, edges, masses, crossings, series, True)
    lane = iota(1, (SHARE, BLOCK))
    held = jnp.zeros((SHARE, BLOCK), jnp.float32)
    width = 2 * PERIODS
    for q in range(width):
        both = series[q // PERIODS, q % PERIODS, :SHARE, :] + series[q // PERIODS, q % PERIODS, SHARE:, :]
        held = jnp.where(lane == q, jnp.sum(both, axis=1, keepdims=True), held)
    for k in range(half_types):
        line = jnp.sum(held[k * BLOCKS : (k + 1) * BLOCKS], axis=0, keepdims=True)
        out[:, k * width : (k + 1) * width] = line[:, :width]


def last_kernel(wanted, price, jac, supply, first_gap, everything, price_out, gap_out, paths_out, *, half_types, all_types):
    width = 2 * PERIODS
    rows = everything.shape[0]
    total = jnp.sum(everything[...], axis=0, keepdims=True)
    assets = total[:, :PERIODS]
    for k in range(1, half_types):
        assets = assets + total[:, k * width : k * width + PERIODS]
    gap = gap_row(assets, supply[...], all_types)
    gap_out[...] = gap
    column = price_column(price[...], jac[...], (first_gap[...], gap))
    price_out[...] = jnp.sum(jnp.where(diagonal(), column, 0.0), axis=0, keepdims=True)
    span = half_types * width
    owner = iota(0, (rows, span)) * half_types + iota(1, (rows, span)) // width
    for s in range(paths_out.shape[0]):
        picked = jnp.where(owner == wanted[pl.ds(s, 1), :span], everything[...], 0.0)
        line = jnp.sum(picked, axis=0, keepdims=True)
        found = line[:, :width]
        for k in range(1, half_types):
            found = found + line[:, k * width : (k + 1) * width]
        for c in range(2):
            paths_out[s, pl.ds(c, 1), :] = found[:, c * PERIODS : (c + 1) * PERIODS]


def body(
    brackets,
    active_blocks,
    initial_mass,
    patience,
    productivity,
    income_levels,
    income_transition,
    wage_path,
    bond_supply,
    price_guess,
    jac_inverse,
    assignment,
):
    local_types = patience.shape[0]
    all_types = local_types * lax.axis_size(TYPES)
    cores = lax.axis_size("tm")
    devices = lax.axis_size(EVERY)
    half_types = local_types // cores
    f32, i32 = jnp.float32, jnp.int32
    by_income = jnp.transpose(brackets, (0, 2, 1, 3)).reshape(cores, half_types, INCOME, HALF, ASSETS)
    theirs = near(lax.ppermute(by_income, "tm", [(c, cores - 1 - c) for c in range(cores)]))

    def exchanged(line):
        copies = jnp.broadcast_to(line[None], (devices, 1, line.shape[1]))
        return near(lax.all_to_all(copies, EVERY, split_axis=0, concat_axis=0, tiled=True).reshape(devices, -1))

    work = [
        pltpu.VMEM((2, PERIODS, BLOCK), f32),
        pltpu.VMEM((PERIODS, ROWS, BLOCK), f32),
        pltpu.VMEM((PERIODS, ROWS, BLOCK), f32),
        pltpu.VMEM((DEEP, BLOCK), f32),
        pltpu.VMEM((DEEP, BLOCK), f32),
        pltpu.VMEM((DEEP, BLOCK), f32),
        pltpu.VMEM((DEEP, BLOCK), f32),
        pltpu.VMEM((2, PERIODS, FRAME, BLOCK), f32),
    ]
    own, *shared, wanted, price_row, jac, supply_row = pl.pallas_call(
        start_kernel,
        name="start",
        out_shape=(
            pltpu.VMEM((HALF, ROWS, BLOCK), i32),
            pltpu.VMEM((ROWS, BLOCK), f32),
            pltpu.VMEM((WAGE + PERIODS, BLOCK), f32),
            pltpu.VMEM((ROWS, BLOCK), f32),
            pltpu.VMEM((ROWS, BLOCK), f32),
            pltpu.VMEM((TILE, BLOCK), i32),
            pltpu.VMEM((1, PERIODS), f32),
            pltpu.VMEM((PERIODS, PERIODS), f32),
            pltpu.VMEM((1, PERIODS), f32),
        ),
        in_specs=[SMEM] * 7 + [VMEM] * 5,
        out_specs=(VMEM,) * 9,
        cost_estimate=pl.CostEstimate(flops=100000, bytes_accessed=2000000, transcendentals=0),
    )(
        active_blocks, patience, productivity, income_levels, income_transition, wage_path, assignment, by_income,
        initial_mass, price_guess.reshape(1, PERIODS), jac_inverse, bond_supply.reshape(1, PERIODS),
    )
    price_row, jac, supply_row = near(price_row), near(jac), near(supply_row)
    shared = [near(array) for array in shared]
    sent, by_row = pl.pallas_call(
        first_kernel,
        name="first_round",
        out_shape=(pltpu.VMEM((1, PERIODS), f32), pltpu.VMEM((PERIODS, ROWS, BLOCK), i32)),
        in_specs=[VMEM] * 7,
        out_specs=(VMEM,) * 2,
        scratch_shapes=work,
    )(near(own), theirs, *shared, price_row)
    totals = exchanged(sent)
    sent, first_gap = pl.pallas_call(
        functools.partial(second_kernel, half_types=half_types, all_types=all_types),
        name="second_round",
        out_shape=(pltpu.VMEM((1, half_types * 2 * PERIODS), f32), pltpu.VMEM((1, PERIODS), f32)),
        in_specs=[VMEM] * 9,
        out_specs=(VMEM,) * 2,
        scratch_shapes=work,
    )(near(by_row), *shared, price_row, jac, supply_row, totals)
    everything = exchanged(sent)
    price_path, market_gap, type_paths = pl.pallas_call(
        functools.partial(last_kernel, half_types=half_types, all_types=all_types),
        name="last_update",
        out_shape=(
            jax.ShapeDtypeStruct((1, PERIODS), f32),
            jax.ShapeDtypeStruct((1, PERIODS), f32),
            jax.ShapeDtypeStruct((local_types, 2, PERIODS), f32),
        ),
        in_specs=[VMEM] * 6,
        out_specs=(VMEM,) * 3,
    )(near(wanted), price_row, jac, supply_row, near(first_gap), everything)
    return price_path.reshape(PERIODS), market_gap.reshape(PERIODS), type_paths


def solution(mesh):
    torus = Mesh(
        mesh.devices.reshape(4, 8, 4, mesh.shape["tm"]), ("types_0", "types_1", "types_2", "tm")
    )
    in_specs = (
        P(TYPES, "tm", None, None),
        P(TYPES),
        P(TYPES, None, None),
        P(TYPES),
        P(TYPES),
        P(),
        P(),
        P(),
        P(),
        P(),
        P(),
        P(),
    )
    out_specs = (P(), P(), P(TYPES, None, None))
    return jax.shard_map(body, mesh=torus, in_specs=in_specs, out_specs=out_specs, check_vma=False)
```

```python
import functools

import jax
import jax.numpy as jnp
from jax import lax
from jax.experimental import pallas as pl
from jax.experimental.pallas import tpu as pltpu
from jax.sharding import Mesh
from jax.sharding import PartitionSpec as P

ASSETS = 512
INCOME = 7
BLOCK = 128
REACH = 8
PERIODS = 8
HALF = PERIODS // 2
BLOCKS = ASSETS // BLOCK
TILE = 8
SHARE = 3 * BLOCKS
LINES = INCOME * SHARE
CHUNKS = -(-LINES // TILE)
ROWS = CHUNKS * TILE
DEEP = ROWS + 2 * TILE
WIDE = 2 * TILE
FRAME = 2 * SHARE
WAGE = 56
TYPES = ("types_0", "types_1", "types_2")
EVERY = ("types_0", "types_1", "types_2", "tm")

grid_top = 40.0
grid_scale = grid_top / (ASSETS - 1) ** 2
rate_floor = 0.005
rate_span = 0.03

VMEM = pl.BlockSpec(memory_space=pltpu.VMEM)
SMEM = pl.BlockSpec(memory_space=pltpu.SMEM)


def near(array):
    return pltpu.with_memory_space_constraint(array, pltpu.VMEM)


def iota(dim, shape=(TILE, BLOCK)):
    return lax.broadcasted_iota(jnp.int32, shape, dim)


def rows_of(chunk):
    return pl.ds(chunk * TILE, TILE)


def splat(row, rows=TILE):
    return jnp.broadcast_to(row, (rows, BLOCK))


def diagonal():
    return iota(0, (PERIODS, PERIODS)) == iota(1, (PERIODS, PERIODS))


def gap_row(totals_row, supply_row, all_types):
    return totals_row * (1.0 / all_types) - supply_row


def price_column(price_row, jac, gaps):
    wide = jnp.where(diagonal(), jnp.broadcast_to(price_row, (PERIODS, PERIODS)), 0.0)
    for gap in gaps:
        wide = wide - jac * gap
    return jnp.sum(wide, axis=1, keepdims=True)


def set_rates(price, rates):
    rate = rate_floor + rate_span / (1.0 + jnp.exp(-price))
    rate = jnp.broadcast_to(rate, (PERIODS, BLOCK))
    rates[0] = rate
    rates[1] = 1.0 / (1.0 + rate)


def pattern():
    first = (iota(0) % BLOCKS) * BLOCK
    point = first + iota(1)
    place = point.astype(jnp.float32)
    return point, first, grid_scale * place * place


def mix(source, target, consts, offset, transposed):
    states = [source(e) for e in range(INCOME)]
    for e in range(INCOME):
        terms = []
        for f in range(INCOME):
            at = f * INCOME + e if transposed else e * INCOME + f
            terms.append(splat(consts[pl.ds(at, 1), :], WIDE) * states[f])
        while len(terms) > 1:
            terms = [sum(terms[i + 1 : i + 2], terms[i]) for i in range(0, len(terms), 2)]
        target[pl.ds(offset + e * SHARE, WIDE), :] = terms[0]


def solve(consts, beta, pay, brackets, start, rates, weights, savings, values, edges, masses, crossings, series, full):
    point, first, grid = pattern()
    lane = iota(1)

    def rate_at(t):
        return splat(rates[0, pl.ds(t, 1), :]), splat(rates[1, pl.ds(t, 1), :])

    def wage_at(t):
        return splat(consts[pl.ds(WAGE + t, 1), :])

    last, _ = rate_at(PERIODS - 1)
    wage = wage_at(PERIODS - 1)
    for c in range(CHUNKS):
        values[rows_of(c), :] = (1.0 + last) / (last * grid + wage * pay[rows_of(c), :])

    def backward(step, carried):
        t = PERIODS - 1 - step
        rate, inverse = rate_at(t)
        wage = wage_at(t)
        budget = (1.0 + rate) * grid
        mix(lambda e: values[pl.ds(e * SHARE, WIDE), :], edges, consts, TILE, False)
        for c in range(CHUNKS):
            line = pl.ds(TILE + c * TILE, TILE)
            income = wage * pay[rows_of(c), :]
            edges[line, :] = (1.0 / (beta[rows_of(c), :] * edges[line, :]) + grid - income) * inverse
        for c in range(CHUNKS):
            income = wage * pay[rows_of(c), :]
            edge = edges[pl.ds(TILE + c * TILE, TILE), :]
            above = edges[pl.ds(TILE + c * TILE - 1, TILE), :]
            bracket = brackets[t, rows_of(c), :]
            spot, after = bracket & (BLOCK - 1), (bracket + 1) & (BLOCK - 1)
            lower = jnp.where(
                bracket >= first,
                jnp.take_along_axis(edge, spot, axis=1),
                jnp.take_along_axis(above, spot, axis=1),
            )
            upper = jnp.where(
                bracket + 1 >= first,
                jnp.take_along_axis(edge, after, axis=1),
                jnp.take_along_axis(above, after, axis=1),
            )
            place = bracket.astype(jnp.float32)
            low = grid_scale * place * place
            width = grid_scale * (2.0 * place + 1.0)
            spacing = jnp.maximum(upper - lower, width * inverse)
            reached = jnp.clip(grid - lower, 0.0, spacing)
            values[rows_of(c), :] = (1.0 + rate) * spacing / ((budget + income - low) * spacing - reached * width)
            weight = reached / spacing
            weights[t, rows_of(c), :] = weight
            savings[t, rows_of(c), :] = low + weight * width
        return carried

    lax.fori_loop(0, PERIODS, backward, 0, unroll=4)
    for c in range(CHUNKS):
        masses[rows_of(c), :] = start[rows_of(c), :]

    def sums(t):
        rate, _ = rate_at(t)
        wage = wage_at(t)
        budget = (1.0 + rate) * grid
        parts = FRAME // TILE
        assets, spent = [None] * parts, [None] * parts
        for c in range(CHUNKS):
            mass, saved = masses[rows_of(c), :], savings[t, rows_of(c), :]
            terms = [mass * saved]
            if full:
                terms.append(mass * (budget + wage * pay[rows_of(c), :] - saved))
            if (c + 1) * TILE > LINES:
                terms = [jnp.where(iota(0) < LINES - c * TILE, term, 0.0) for term in terms]
            for held, term in zip((assets, spent), terms):
                held[c % parts] = term if held[c % parts] is None else held[c % parts] + term
        for q, held in enumerate((assets, spent) if full else (assets,)):
            for part in range(parts):
                series[q, t, pl.ds(part * TILE, TILE), :] = held[part]

    def forward(t, carried):
        sums(t)
        for c in range(CHUNKS):
            mass, weight = masses[rows_of(c), :], weights[t, rows_of(c), :]
            rising = weight * mass
            staying = (1.0 - weight) * mass
            drop = point - brackets[t, rows_of(c), :]
            hit = [drop == s for s in range(REACH + 2)]
            here = jnp.where(hit[0], staying, jnp.where(hit[1], rising, 0.0))
            here = here + pltpu.roll(jnp.where(hit[0], rising, 0.0), 1, 1)
            parts = []
            for s in range(1, REACH + 2):
                moved = jnp.where(hit[s], staying, jnp.where(hit[s + 1], rising, 0.0) if s <= REACH else 0.0)
                moved = pltpu.roll(moved, BLOCK - s, 1)
                inside = lane < BLOCK - s
                parts.append((jnp.where(inside, moved, 0.0), jnp.where(inside, 0.0, moved)))
            while len(parts) > 1:
                parts = [tuple(sum(z[1:], z[0]) for z in zip(*parts[i : i + 2])) for i in range(0, len(parts), 2)]
            here, crossed = here + parts[0][0], parts[0][1]
            edges[rows_of(c), :] = here
            crossings[rows_of(c), :] = crossed

        def arrived(e):
            return edges[pl.ds(e * SHARE, WIDE), :] + crossings[pl.ds(e * SHARE + 1, WIDE), :]

        mix(arrived, masses, consts, 0, True)
        return carried

    lax.fori_loop(0, PERIODS - 1, forward, 0, unroll=True)
    sums(PERIODS - 1)


def start_kernel(
    blocks, patience, productivity, levels, transition, wage, assignment, mine, mass, price_in, jac_in, supply_in,
    own, start, consts, beta, pay, wanted, price, jac, supply, rates,
):
    price[...], jac[...], supply[...] = price_in[...], jac_in[...], supply_in[...]
    set_rates(price_column(price_in[...], None, ()), rates)
    half_types = mine.shape[1]
    core = lax.axis_index("tm")
    here = lax.axis_index(TYPES)
    for e in range(INCOME):
        for f in range(INCOME):
            consts[e * INCOME + f : e * INCOME + f + 1, :] = jnp.full((1, BLOCK), transition[e, f], jnp.float32)
    for t in range(PERIODS):
        consts[WAGE + t : WAGE + t + 1, :] = jnp.full((1, BLOCK), wage[t], jnp.float32)
    for s in range(TILE):
        slot = here * 2 * half_types + min(s, 2 * half_types - 1)
        wanted[s : s + 1, :] = jnp.full((1, BLOCK), assignment[slot], jnp.int32)
    for k in range(half_types):
        alive = blocks[core * half_types + k]
        patient, skill = patience[core * half_types + k], productivity[core * half_types + k]
        for e in range(INCOME):
            top = e * SHARE + k * BLOCKS
            beta[top : top + BLOCKS, :] = jnp.full((BLOCKS, BLOCK), patient, jnp.float32)
            pay[top : top + BLOCKS, :] = jnp.full((BLOCKS, BLOCK), skill * levels[e], jnp.float32)
            for b in range(BLOCKS):
                line, part = pl.ds(top + b, 1), pl.ds(b * BLOCK, BLOCK)
                live = (b < alive).astype(jnp.float32)
                start[line, :] = mass[core * half_types + k, pl.ds(e, 1), part] * live
                for t in range(HALF):
                    own[t, line, :] = mine[core, k, e, pl.ds(t, 1), part]
    spare = ROWS - LINES
    beta[LINES:, :] = jnp.ones((spare, BLOCK), jnp.float32)
    pay[LINES:, :] = jnp.ones((spare, BLOCK), jnp.float32)
    start[LINES:, :] = jnp.zeros((spare, BLOCK), jnp.float32)
    for t in range(HALF):
        own[t, LINES:, :] = jnp.zeros((spare, BLOCK), jnp.int32)


def first_kernel(
    own, theirs, start, consts, beta, pay, rates,
    out, brackets, weights, savings, values, edges, masses, crossings, series,
):
    half_types = theirs.shape[1]
    core = lax.axis_index("tm")
    for t in range(HALF):
        brackets[core * HALF + t] = own[t]
        brackets[(1 - core) * HALF + t, LINES:, :] = jnp.zeros((ROWS - LINES, BLOCK), jnp.int32)
    for k in range(half_types):
        for e in range(INCOME):
            for b in range(BLOCKS):
                line, part = pl.ds(e * SHARE + k * BLOCKS + b, 1), pl.ds(b * BLOCK, BLOCK)
                for t in range(HALF):
                    brackets[(1 - core) * HALF + t, line, :] = theirs[core, k, e, pl.ds(t, 1), part]
    solve(consts, beta, pay, brackets, start, rates, weights, savings, values, edges, masses, crossings, series, False)
    lane = iota(1)
    held = jnp.zeros((TILE, BLOCK), jnp.float32)
    for t in range(PERIODS):
        total = series[0, t, :TILE, :]
        for part in range(1, FRAME // TILE):
            total = total + series[0, t, part * TILE : (part + 1) * TILE, :]
        held = jnp.where(lane == t, jnp.sum(total, axis=1, keepdims=True), held)
    out[...] = jnp.sum(held, axis=0, keepdims=True)[:, :PERIODS]


def second_kernel(
    brackets, start, consts, beta, pay, price, jac, supply, totals,
    out, gap_out, rates, weights, savings, values, edges, masses, crossings, series,
    *, half_types, all_types,
):
    total = jnp.sum(totals[...], axis=0, keepdims=True)
    gap = gap_row(total, supply[...], all_types)
    gap_out[...] = gap
    set_rates(price_column(price[...], jac[...], (gap,)), rates)
    solve(consts, beta, pay, brackets, start, rates, weights, savings, values, edges, masses, crossings, series, True)
    lane = iota(1, (SHARE, BLOCK))
    held = jnp.zeros((SHARE, BLOCK), jnp.float32)
    width = 2 * PERIODS
    for q in range(width):
        both = series[q // PERIODS, q % PERIODS, :SHARE, :] + series[q // PERIODS, q % PERIODS, SHARE:, :]
        held = jnp.where(lane == q, jnp.sum(both, axis=1, keepdims=True), held)
    for k in range(half_types):
        line = jnp.sum(held[k * BLOCKS : (k + 1) * BLOCKS], axis=0, keepdims=True)
        out[:, k * width : (k + 1) * width] = line[:, :width]


def last_kernel(wanted, price, jac, supply, first_gap, everything, price_out, gap_out, paths_out, *, half_types, all_types):
    width = 2 * PERIODS
    rows = everything.shape[0]
    total = jnp.sum(everything[...], axis=0, keepdims=True)
    assets = total[:, :PERIODS]
    for k in range(1, half_types):
        assets = assets + total[:, k * width : k * width + PERIODS]
    gap = gap_row(assets, supply[...], all_types)
    gap_out[...] = gap
    column = price_column(price[...], jac[...], (first_gap[...], gap))
    price_out[...] = jnp.sum(jnp.where(diagonal(), column, 0.0), axis=0, keepdims=True)
    span = half_types * width
    owner = iota(0, (rows, span)) * half_types + iota(1, (rows, span)) // width
    for s in range(paths_out.shape[0]):
        picked = jnp.where(owner == wanted[pl.ds(s, 1), :span], everything[...], 0.0)
        line = jnp.sum(picked, axis=0, keepdims=True)
        found = line[:, :width]
        for k in range(1, half_types):
            found = found + line[:, k * width : (k + 1) * width]
        for c in range(2):
            paths_out[s, pl.ds(c, 1), :] = found[:, c * PERIODS : (c + 1) * PERIODS]


def body(
    brackets,
    active_blocks,
    initial_mass,
    patience,
    productivity,
    income_levels,
    income_transition,
    wage_path,
    bond_supply,
    price_guess,
    jac_inverse,
    assignment,
):
    local_types = patience.shape[0]
    all_types = local_types * lax.axis_size(TYPES)
    cores = lax.axis_size("tm")
    devices = lax.axis_size(EVERY)
    half_types = local_types // cores
    f32, i32 = jnp.float32, jnp.int32
    by_income = jnp.transpose(brackets, (0, 2, 1, 3)).reshape(cores, half_types, INCOME, HALF, ASSETS)
    theirs = near(lax.ppermute(by_income, "tm", [(c, cores - 1 - c) for c in range(cores)]))

    def exchanged(line):
        copies = jnp.broadcast_to(line[None], (devices, 1, line.shape[1]))
        return near(lax.all_to_all(copies, EVERY, split_axis=0, concat_axis=0, tiled=True).reshape(devices, -1))

    work = [
        pltpu.VMEM((2, PERIODS, BLOCK), f32),
        pltpu.VMEM((PERIODS, ROWS, BLOCK), f32),
        pltpu.VMEM((PERIODS, ROWS, BLOCK), f32),
        pltpu.VMEM((DEEP, BLOCK), f32),
        pltpu.VMEM((DEEP, BLOCK), f32),
        pltpu.VMEM((DEEP, BLOCK), f32),
        pltpu.VMEM((DEEP, BLOCK), f32),
        pltpu.VMEM((2, PERIODS, FRAME, BLOCK), f32),
    ]
    own, *shared, wanted, price_row, jac, supply_row, first_rates = pl.pallas_call(
        start_kernel,
        name="start",
        out_shape=(
            pltpu.VMEM((HALF, ROWS, BLOCK), i32),
            pltpu.VMEM((ROWS, BLOCK), f32),
            pltpu.VMEM((WAGE + PERIODS, BLOCK), f32),
            pltpu.VMEM((ROWS, BLOCK), f32),
            pltpu.VMEM((ROWS, BLOCK), f32),
            pltpu.VMEM((TILE, BLOCK), i32),
            pltpu.VMEM((1, PERIODS), f32),
            pltpu.VMEM((PERIODS, PERIODS), f32),
            pltpu.VMEM((1, PERIODS), f32),
            pltpu.VMEM((2, PERIODS, BLOCK), f32),
        ),
        in_specs=[SMEM] * 7 + [VMEM] * 5,
        out_specs=(VMEM,) * 10,
        cost_estimate=pl.CostEstimate(flops=100000, bytes_accessed=2000000, transcendentals=0),
    )(
        active_blocks, patience, productivity, income_levels, income_transition, wage_path, assignment, by_income,
        initial_mass, price_guess.reshape(1, PERIODS), jac_inverse, bond_supply.reshape(1, PERIODS),
    )
    price_row, jac, supply_row = near(price_row), near(jac), near(supply_row)
    shared = [near(array) for array in shared]
    sent, by_row = pl.pallas_call(
        first_kernel,
        name="first_round",
        out_shape=(pltpu.VMEM((1, PERIODS), f32), pltpu.VMEM((PERIODS, ROWS, BLOCK), i32)),
        in_specs=[VMEM] * 7,
        out_specs=(VMEM,) * 2,
        scratch_shapes=work[1:],
    )(near(own), theirs, *shared, near(first_rates))
    totals = exchanged(sent)
    sent, first_gap = pl.pallas_call(
        functools.partial(second_kernel, half_types=half_types, all_types=all_types),
        name="second_round",
        out_shape=(pltpu.VMEM((1, half_types * 2 * PERIODS), f32), pltpu.VMEM((1, PERIODS), f32)),
        in_specs=[VMEM] * 9,
        out_specs=(VMEM,) * 2,
        scratch_shapes=work,
    )(near(by_row), *shared, price_row, jac, supply_row, totals)
    everything = exchanged(sent)
    price_path, market_gap, type_paths = pl.pallas_call(
        functools.partial(last_kernel, half_types=half_types, all_types=all_types),
        name="last_update",
        out_shape=(
            jax.ShapeDtypeStruct((1, PERIODS), f32),
            jax.ShapeDtypeStruct((1, PERIODS), f32),
            jax.ShapeDtypeStruct((local_types, 2, PERIODS), f32),
        ),
        in_specs=[VMEM] * 6,
        out_specs=(VMEM,) * 3,
    )(near(wanted), price_row, jac, supply_row, near(first_gap), everything)
    return price_path.reshape(PERIODS), market_gap.reshape(PERIODS), type_paths


def solution(mesh):
    torus = Mesh(
        mesh.devices.reshape(4, 8, 4, mesh.shape["tm"]), ("types_0", "types_1", "types_2", "tm")
    )
    in_specs = (
        P(TYPES, "tm", None, None),
        P(TYPES),
        P(TYPES, None, None),
        P(TYPES),
        P(TYPES),
        P(),
        P(),
        P(),
        P(),
        P(),
        P(),
        P(),
    )
    out_specs = (P(), P(), P(TYPES, None, None))
    return jax.shard_map(body, mesh=torus, in_specs=in_specs, out_specs=out_specs, check_vma=False)
```
